1024 devices in a mesh: pipe: 64 (over y_lo, z), tensor: 16 (over x, y_hi, core).
Axes of the slice: x: 4, y: 4 (y_hi: 2, y_lo: 2; y = y_hi * 2 + y_lo), z: 32, core: 2. Of those that a mesh axis runs over, the one named last changes fastest.
Arguments:
- residual: bfloat16 [64, 128, 4096], P('pipe'), may hold values from -4 to 4
- out_proj: bfloat16 [64, 4096, 4096], P('pipe', 'tensor'), may hold values from -0.25 to 0.25
- attn_in: bfloat16 [64, 3, 128, 4096], P('pipe', None, None, 'tensor'), may hold values from -9 to 9
- stash_slots: bfloat16 [64, 2, 3, 128, 4096], P('pipe', None, None, None, 'tensor'), may hold values from -9 to 9
- grad_in: bfloat16 [64, 128, 4096], P('pipe'), may hold values from -6 to 6
- stash_slot: int32 [64], replicated, may hold values from 0 to 1
Outputs:
- fwd_out: bfloat16 [64, 128, 4096], P('pipe')
- qkv_grad: bfloat16 [64, 3, 128, 4096], P('pipe', None, None, 'tensor')
- evicted: bfloat16 [64, 3, 128, 4096], P('pipe', None, None, 'tensor')
The draws below stay inside these ranges and needn't reach their ends.
All inputs are finite; a program needn't handle non-finite values.
Results may differ from the reference program's by a relative error of at most 0.0065.
Values may be sent and summed in bfloat16 or wider, within the bound.
No kernel may reach another device: no remote copies, remote signals or barrier semaphores. Data moves between devices by JAX's collectives and lax.ppermute only.
A program may use at most 32 MiB of HBM per device.

```python
import jax
import jax.numpy as jnp
from jax import lax

D = 4096
HD = 128
HEADS = 32
ROWS = 128
SLOTS = 2
SECTIONS = 64


def attention_law(key, leading):
    full_shape = leading + (3, ROWS, HEADS * HD)
    return jnp.clip(jax.random.normal(key, full_shape, jnp.float32), -6.0, 6.0)


def draw_attn_in(key, part):
    return attention_law(jax.random.fold_in(key, 1), (SECTIONS,)).astype(jnp.bfloat16)


def draw_stash_slots(key, part):
    return attention_law(jax.random.fold_in(key, 2), (SECTIONS, SLOTS)).astype(jnp.bfloat16)


def touch_ends(values, own_key, smallest, largest):
    spot = [jax.random.randint(jax.random.fold_in(own_key, axis), (), 0, length) for axis, length in enumerate(values.shape)]
    longest = values.shape.index(max(values.shape))
    next_to = spot[:longest] + [(spot[longest] + 1) % values.shape[longest]] + spot[longest + 1:]
    return values.at[tuple(spot)].set(smallest).at[tuple(next_to)].set(largest)


def shard_levels(key, shape, pieces, smallest, top_value):
    level = 1.0
    for position, parts in pieces:
        steps = jax.random.uniform(jax.random.fold_in(jax.random.fold_in(key, 6), position), (parts,), jnp.float32, smallest / len(pieces), top_value / len(pieces))
        level = level * jnp.repeat(jnp.exp(steps), shape[position] // parts).reshape((-1,) + (1,) * (len(shape) - 1 - position))
    return level


def normal_values(key, extent, deviation, bound, pieces=(), kind=jnp.bfloat16):
    result = jax.random.normal(key, extent, jnp.float32) * deviation
    if len(pieces) > 0:
        result = shard_levels(key, extent, pieces, -0.22, 0.18) * result
    return jnp.clip(result, min=-bound, max=bound).astype(kind)


def setup_inputs(seed: int = 0) -> dict:
    streams_of = jax.random.split(jax.random.key(seed), 7)
    residual = normal_values(streams_of[0], (SECTIONS, ROWS, D), 0.3, 4.0, ((0, 64),))
    out_proj = normal_values(streams_of[1], (SECTIONS, HEADS * HD, D), (HEADS * HD // 8) ** -0.5, 0.25, ((0, 64), (1, 16)))
    attn_in = draw_attn_in(jax.random.fold_in(streams_of[6], 71), 0)
    stash_slots = draw_stash_slots(jax.random.fold_in(streams_of[6], 71), 0)
    grad_in = normal_values(streams_of[4], (SECTIONS, ROWS, D), 1.0, 6.0, ((0, 64),))
    stash_slot = touch_ends(jax.random.randint(streams_of[5], (SECTIONS,), 0, SLOTS), jax.random.fold_in(streams_of[5], 1), 0, SLOTS - 1).astype(jnp.int32)
    return dict(residual=residual, out_proj=out_proj, attn_in=attn_in, stash_slots=stash_slots, grad_in=grad_in, stash_slot=stash_slot)


def head_probs(query_in, key_in):
    length = query_in.shape[0]
    query_heads = query_in.astype(jnp.float32).reshape(length, -1, HD)
    key_heads = key_in.astype(jnp.float32).reshape(length, -1, HD)
    scores = jnp.einsum("ihd,jhd->hij", query_heads, key_heads) * (HD ** -0.5)
    row_ids = jnp.arange(length, dtype=jnp.int32)
    allowed = row_ids[:, None] >= row_ids[None, :]
    scores = jnp.where(allowed[None], scores, -jnp.inf)
    return jax.nn.softmax(scores, axis=-1)


def attend(inputs):
    length = inputs.shape[1]
    attn_probs = head_probs(inputs[0], inputs[1])
    probs_low = lax.optimization_barrier(attn_probs.astype(jnp.bfloat16)).astype(jnp.float32)
    value_heads = inputs[2].astype(jnp.float32).reshape(length, -1, HD)
    context = jnp.einsum("hij,jhd->ihd", probs_low, value_heads)
    return context.reshape(length, -1).astype(jnp.bfloat16)


def attend_back(stored, grad_context):
    length = stored.shape[1]
    scale_factor = HD ** -0.5
    attn_probs = head_probs(stored[0], stored[1])
    grad_heads = lax.optimization_barrier(grad_context).astype(jnp.float32).reshape(length, -1, HD)
    query_heads = stored[0].astype(jnp.float32).reshape(length, -1, HD)
    key_heads = stored[1].astype(jnp.float32).reshape(length, -1, HD)
    value_heads = stored[2].astype(jnp.float32).reshape(length, -1, HD)
    grad_probs = jnp.einsum("ihd,jhd->hij", grad_heads, value_heads)
    row_delta = jnp.sum(attn_probs * grad_probs, axis=-1, keepdims=True)
    grad_scores = (attn_probs * (grad_probs - row_delta)).astype(jnp.bfloat16)
    grad_scores = lax.optimization_barrier(grad_scores).astype(jnp.float32)
    probs_low = lax.optimization_barrier(attn_probs.astype(jnp.bfloat16)).astype(jnp.float32)
    grad_query = jnp.einsum("hij,jhd->ihd", grad_scores, key_heads) * scale_factor
    grad_key = jnp.einsum("hij,ihd->jhd", grad_scores, query_heads) * scale_factor
    grad_value = jnp.einsum("hij,ihd->jhd", probs_low, grad_heads)
    stacked = jnp.stack([grad_query, grad_key, grad_value], axis=0)
    return stacked.reshape(3, length, -1).astype(jnp.bfloat16)


def forward_section(inputs, resid_rows, weight):
    context = attend(inputs)
    branch = jnp.dot(context, weight, preferred_element_type=jnp.float32)
    return (resid_rows.astype(jnp.float32) + branch).astype(jnp.bfloat16)


def backward_section(stored, grad_rows, weight):
    grad_context = lax.dot_general(grad_rows, weight, (((1,), (1,)), ((), ())), preferred_element_type=jnp.float32)
    return attend_back(stored, grad_context.astype(jnp.bfloat16))


def reference(residual, out_proj, attn_in, stash_slots, grad_in, stash_slot):
    section_ids = jnp.arange(SECTIONS, dtype=jnp.int32)
    partner = ((section_ids + SECTIONS // 2) % SECTIONS).astype(jnp.int32)
    section_outs = lax.map(lambda items: forward_section(items[0], items[1], items[2]), (attn_in, residual, out_proj))
    fwd_out = jnp.roll(section_outs, 1, axis=0)
    stored = stash_slots[partner, stash_slot]
    all_grads = lax.map(lambda items: backward_section(items[0], items[1], items[2]), (stored, grad_in, out_proj))
    evicted = attn_in[partner]
    return fwd_out, all_grads, evicted
```

```python
import jax
import jax.numpy as jnp
from jax import lax
from jax.experimental import pallas as pl
from jax.experimental.pallas import tpu as pltpu
from jax.sharding import PartitionSpec as P


HD = 128
SCALE = HD ** (-0.5)
BF = jnp.bfloat16
F32 = jnp.float32
VMEM = pl.BlockSpec(memory_space=pltpu.VMEM)
SMEM = pl.BlockSpec(memory_space=pltpu.SMEM)
ANY = pl.BlockSpec(memory_space=pl.ANY)


def struct(shape, dtype=BF):
    return jax.ShapeDtypeStruct(shape, dtype)


def dot(a, b, ca, cb):
    return lax.dot_general(a, b, (((ca,), (cb,)), ((), ())), preferred_element_type=F32)


def probs_of(query, key):
    scores = dot(query, key, 1, 1) * SCALE
    rows = lax.broadcasted_iota(jnp.int32, scores.shape, 0)
    cols = lax.broadcasted_iota(jnp.int32, scores.shape, 1)
    scores = jnp.where(rows >= cols, scores, -jnp.inf)
    top = jnp.max(scores, axis=1, keepdims=True)
    weights = jnp.exp(scores - top)
    return weights / jnp.sum(weights, axis=1, keepdims=True)


def forward_kernel(qkv_hbm, weight_hbm, out_hbm, qkv, weight, out, sems):
    tiles, tile = weight.shape[0], weight.shape[2]
    head_count = qkv.shape[2] // HD
    load_qkv = pltpu.make_async_copy(qkv_hbm.at[0], qkv, sems.at[0])
    loads, stores = [], []
    for n in range(tiles):
        c = slice(n * tile, (n + 1) * tile)
        loads.append(pltpu.make_async_copy(weight_hbm.at[0, :, c], weight.at[n], sems.at[1 + n]))
        stores.append(pltpu.make_async_copy(out.at[n], out_hbm.at[:, c], sems.at[1 + tiles + n]))
    load_qkv.start()
    for load in loads:
        load.start()
    load_qkv.wait()
    heads = []
    for h in range(head_count):
        c = slice(h * HD, (h + 1) * HD)
        probs = probs_of(qkv[0, :, c], qkv[1, :, c]).astype(BF)
        heads.append(dot(probs, qkv[2, :, c], 1, 0).astype(BF))
    context = jnp.concatenate(heads, axis=1)
    for n in range(tiles):
        loads[n].wait()
        out[n] = dot(context, weight[n], 1, 0).astype(BF)
        stores[n].start()
    for store in stores:
        store.wait()


def pick_kernel(slots, stash, qkv, residual, pair, rows, sems):
    sections = lax.axis_size("pipe")
    partner = lax.rem(lax.axis_index("pipe") + sections // 2, sections)
    share = rows.shape[0]
    first = pl.multiple_of(lax.axis_index("tensor") * share, share)
    copies = (
        pltpu.make_async_copy(stash.at[0, slots[partner]], pair.at[0], sems.at[0]),
        pltpu.make_async_copy(qkv.at[0], pair.at[1], sems.at[1]),
        pltpu.make_async_copy(residual.at[0, pl.ds(first, share)], rows, sems.at[2]),
    )
    for copy in copies:
        copy.start()
    for copy in copies:
        copy.wait()


def backward_kernel(pair, grad_context, grads, evicted):
    for h in range(grad_context.shape[1] // HD):
        c = slice(h * HD, (h + 1) * HD)
        query, key, value = pair[0, 0, :, c], pair[0, 1, :, c], pair[0, 2, :, c]
        grad = grad_context[:, c]
        probs = probs_of(query, key)
        grad_probs = dot(grad, value, 1, 1)
        delta = jnp.sum(probs * grad_probs, axis=1, keepdims=True)
        grad_scores = (probs * (grad_probs - delta)).astype(BF)
        grads[0, 0, :, c] = (dot(grad_scores, key, 1, 0) * SCALE).astype(BF)
        grads[0, 1, :, c] = (dot(grad_scores, query, 0, 0) * SCALE).astype(BF)
        grads[0, 2, :, c] = dot(probs.astype(BF), grad, 0, 0).astype(BF)
    evicted[0] = pair[1]


def shifted(block, axis, distance):
    count = lax.axis_size(axis)
    return lax.ppermute(block, axis, [((i - distance) % count, i) for i in range(count)])


def step(residual, out_proj, attn_in, stash_slots, grad_in, stash_slot):
    sections, members = lax.axis_size("pipe"), lax.axis_size("tensor")
    weight = out_proj[0]
    rows, width = residual.shape[1:]
    share = rows // members
    tiles = 4
    partial = pl.pallas_call(
        forward_kernel,
        out_shape=struct((rows, width)),
        in_specs=[ANY, ANY],
        out_specs=ANY,
        scratch_shapes=[
            pltpu.VMEM(attn_in.shape[1:], BF),
            pltpu.VMEM((tiles, weight.shape[0], width // tiles), BF),
            pltpu.VMEM((tiles, rows, width // tiles), BF),
            pltpu.SemaphoreType.DMA((1 + 2 * tiles,)),
        ],
        name="front",
    )(attn_in, out_proj)
    parts = lax.all_to_all(partial.reshape(members, share, width), "tensor", 0, 0, tiled=True)
    pair, own_rows = pl.pallas_call(
        pick_kernel,
        out_shape=(struct((2, *attn_in.shape[1:])), struct((share, width))),
        in_specs=[SMEM, ANY, ANY, ANY],
        out_specs=(VMEM, VMEM),
        scratch_shapes=[pltpu.SemaphoreType.DMA((3,))],
        name="pick",
    )(stash_slot, stash_slots, attn_in, residual)
    swapped = shifted(pair, "pipe", sections // 2)
    grad_context = dot(grad_in[0], weight, 1, 1).astype(BF)
    own = (own_rows.astype(F32) + jnp.sum(parts.astype(F32), axis=0)).astype(BF)
    moved = shifted(own, "pipe", 1)
    copies = jnp.broadcast_to(moved[None], (members, share, width))
    arrived = lax.all_to_all(copies, "tensor", 0, 0, tiled=True)
    qkv_grad, evicted = pl.pallas_call(
        backward_kernel,
        out_shape=(struct(attn_in.shape), struct(attn_in.shape)),
        in_specs=[VMEM, VMEM],
        out_specs=(VMEM, VMEM),
        name="back",
        compiler_params=pltpu.CompilerParams(vmem_limit_bytes=4 << 20),
    )(swapped, grad_context)
    return arrived.reshape(1, rows, width), qkv_grad, evicted


def solution(mesh):
    in_specs = (
        P("pipe", None, None),
        P("pipe", "tensor", None),
        P("pipe", None, None, "tensor"),
        P("pipe", None, None, None, "tensor"),
        P("pipe", None, None),
        P(),
    )
    out_specs = (
        P("pipe", None, None),
        P("pipe", None, None, "tensor"),
        P("pipe", None, None, "tensor"),
    )
    return jax.shard_map(step, mesh=mesh, in_specs=in_specs, out_specs=out_specs, check_vma=False)
```

```python
import functools

import jax
import jax.numpy as jnp
from jax import lax
from jax.experimental import pallas as pl
from jax.experimental.pallas import tpu as pltpu
from jax.sharding import PartitionSpec as P


HD = 128
SCALE = HD ** (-0.5)
BF = jnp.bfloat16
F32 = jnp.float32
VMEM = pl.BlockSpec(memory_space=pltpu.VMEM)
SMEM = pl.BlockSpec(memory_space=pltpu.SMEM)
ANY = pl.BlockSpec(memory_space=pl.ANY)
SMALL = pltpu.CompilerParams(vmem_limit_bytes=4 << 20)


def struct(shape, dtype=BF):
    return jax.ShapeDtypeStruct(shape, dtype)


def dot(a, b, ca, cb):
    return lax.dot_general(a, b, (((ca,), (cb,)), ((), ())), preferred_element_type=F32)


def core_of_chip():
    return lax.rem(lax.axis_index("tensor"), 2)


def probs_of(query, key):
    scores = dot(query, key, 1, 1) * SCALE
    rows = lax.broadcasted_iota(jnp.int32, scores.shape, 0)
    cols = lax.broadcasted_iota(jnp.int32, scores.shape, 1)
    scores = jnp.where(rows >= cols, scores, -jnp.inf)
    top = jnp.max(scores, axis=1, keepdims=True)
    weights = jnp.exp(scores - top)
    return weights / jnp.sum(weights, axis=1, keepdims=True)


def forward_kernel(qkv_hbm, weight_hbm, own_context, out_hbm, qkv, weight, context, out, sems):
    tiles, tile = weight.shape[0], weight.shape[2]
    half = own_context.shape[0]
    load_qkv = pltpu.make_async_copy(qkv_hbm.at[0], qkv, sems.at[0])
    loads, stores = [], []
    for n in range(tiles):
        c = slice(n * tile, (n + 1) * tile)
        loads.append(pltpu.make_async_copy(weight_hbm.at[0, :, c], weight.at[n], sems.at[1 + n]))
        stores.append(pltpu.make_async_copy(out.at[n], out_hbm.at[:, c], sems.at[1 + tiles + n]))
    load_qkv.start()
    for load in loads:
        load.start()
    load_qkv.wait()
    for h in range(qkv.shape[2] // HD):
        c = slice(h * HD, (h + 1) * HD)
        probs = probs_of(qkv[0, :, c], qkv[1, :, c]).astype(BF)
        context[:, c] = dot(probs, qkv[2, :, c], 1, 0).astype(BF)
    core = core_of_chip()
    own_context[...] = context[pl.ds(pl.multiple_of(core * half, half), half), :]
    theirs = context[pl.ds(pl.multiple_of((1 - core) * half, half), half), :]
    for n in range(tiles):
        loads[n].wait()
        out[n] = dot(theirs, weight[n], 1, 0).astype(BF)
        stores[n].start()
    for store in stores:
        store.wait()


def pick_kernel(slots, stash, qkv, residual, pair, rows, sems):
    sections = lax.axis_size("pipe")
    partner = lax.rem(lax.axis_index("pipe") + sections // 2, sections)
    share = rows.shape[0]
    half = residual.shape[1] // 2
    first = core_of_chip() * half + lax.div(lax.axis_index("tensor"), 2) * share
    first = pl.multiple_of(first, share)
    copies = (
        pltpu.make_async_copy(stash.at[0, slots[partner]], pair.at[0], sems.at[0]),
        pltpu.make_async_copy(qkv.at[0], pair.at[1], sems.at[1]),
        pltpu.make_async_copy(residual.at[0, pl.ds(first, share)], rows, sems.at[2]),
    )
    for copy in copies:
        copy.start()
    for copy in copies:
        copy.wait()


def place_kernel(other, block, *refs):
    out, sem = refs[-2:]
    half = block.shape[0]
    core = core_of_chip()
    first = pl.multiple_of((1 - core if other else core) * half, half)
    copy = pltpu.make_async_copy(block, out.at[0, pl.ds(first, half)], sem)
    copy.start()
    copy.wait()


def backward_kernel(pair, grad_context, grads, evicted):
    for h in range(grad_context.shape[1] // HD):
        c = slice(h * HD, (h + 1) * HD)
        query, key, value = pair[0, 0, :, c], pair[0, 1, :, c], pair[0, 2, :, c]
        grad = grad_context[:, c]
        probs = probs_of(query, key)
        grad_probs = dot(grad, value, 1, 1)
        delta = jnp.sum(probs * grad_probs, axis=1, keepdims=True)
        grad_scores = (probs * (grad_probs - delta)).astype(BF)
        grads[0, 0, :, c] = (dot(grad_scores, key, 1, 0) * SCALE).astype(BF)
        grads[0, 1, :, c] = (dot(grad_scores, query, 0, 0) * SCALE).astype(BF)
        grads[0, 2, :, c] = dot(probs.astype(BF), grad, 0, 0).astype(BF)
    evicted[0] = pair[1]


def shifted(block, axis, distance):
    count = lax.axis_size(axis)
    return lax.ppermute(block, axis, [((i - distance) % count, i) for i in range(count)])


def crossed(block):
    return lax.ppermute(block, "tensor", [(i, i ^ 1) for i in range(lax.axis_size("tensor"))])


def exchanged(blocks):
    members = lax.axis_size("tensor")
    groups = [list(range(core, members, 2)) for core in range(2)]
    return lax.all_to_all(blocks, "tensor", 0, 0, axis_index_groups=groups, tiled=True)


def step(residual, out_proj, attn_in, stash_slots, grad_in, stash_slot):
    sections, members = lax.axis_size("pipe"), lax.axis_size("tensor")
    weight = out_proj[0]
    rows, width = residual.shape[1:]
    chips, half, share = members // 2, rows // 2, rows // members
    tiles = 4
    own_context, product = pl.pallas_call(
        forward_kernel,
        out_shape=(struct((half, weight.shape[0])), struct((half, width))),
        in_specs=[ANY, ANY],
        out_specs=(VMEM, ANY),
        scratch_shapes=[
            pltpu.VMEM(attn_in.shape[1:], BF),
            pltpu.VMEM((tiles, weight.shape[0], width // tiles), BF),
            pltpu.VMEM((rows, weight.shape[0]), BF),
            pltpu.VMEM((tiles, half, width // tiles), BF),
            pltpu.SemaphoreType.DMA((1 + 2 * tiles,)),
        ],
        name="front",
    )(attn_in, out_proj)
    received = crossed(product)
    own = dot(own_context, weight, 1, 0)
    partial = (own + received.astype(F32)).astype(BF).reshape(chips, share, width)
    parts = exchanged(partial)
    pair, own_rows = pl.pallas_call(
        pick_kernel,
        out_shape=(struct((2, *attn_in.shape[1:])), struct((share, width))),
        in_specs=[SMEM, ANY, ANY, ANY],
        out_specs=(VMEM, VMEM),
        scratch_shapes=[pltpu.SemaphoreType.DMA((3,))],
        name="pick",
    )(stash_slot, stash_slots, attn_in, residual)
    swapped = shifted(pair, "pipe", sections // 2)
    grad_context = dot(grad_in[0], weight, 1, 1).astype(BF)
    total = own_rows.astype(F32)
    for chip in range(chips):
        total = total + parts[chip].astype(F32)
    total = total.astype(BF)
    moved = shifted(total, "pipe", 1)
    copies = jnp.broadcast_to(moved[None], (chips, share, width))
    arrived = exchanged(copies).reshape(half, width)
    qkv_grad, evicted = pl.pallas_call(
        backward_kernel,
        out_shape=(struct(attn_in.shape), struct(attn_in.shape)),
        in_specs=[VMEM, VMEM],
        out_specs=(VMEM, VMEM),
        compiler_params=SMALL,
        name="back",
    )(swapped, grad_context)
    other = crossed(arrived)
    placed = pl.pallas_call(
        functools.partial(place_kernel, False),
        out_shape=struct(residual.shape),
        in_specs=[VMEM],
        out_specs=ANY,
        scratch_shapes=[pltpu.SemaphoreType.DMA],
        compiler_params=SMALL,
        name="place",
    )(arrived)
    fwd_out = pl.pallas_call(
        functools.partial(place_kernel, True),
        out_shape=struct(residual.shape),
        in_specs=[VMEM, ANY],
        out_specs=ANY,
        input_output_aliases={1: 0},
        scratch_shapes=[pltpu.SemaphoreType.DMA],
        compiler_params=SMALL,
        name="join",
    )(other, placed)
    return fwd_out, qkv_grad, evicted


def solution(mesh):
    in_specs = (
        P("pipe", None, None),
        P("pipe", "tensor", None),
        P("pipe", None, None, "tensor"),
        P("pipe", None, None, None, "tensor"),
        P("pipe", None, None),
        P(),
    )
    out_specs = (
        P("pipe", None, None),
        P("pipe", None, None, "tensor"),
        P("pipe", None, None, "tensor"),
    )
    return jax.shard_map(step, mesh=mesh, in_specs=in_specs, out_specs=out_specs, check_vma=False)
```

```python
import functools

import jax
import jax.numpy as jnp
from jax import lax
from jax.experimental import pallas as pl
from jax.experimental.pallas import tpu as pltpu
from jax.sharding import PartitionSpec as P


HD = 128
SCALE = HD ** (-0.5)
BF = jnp.bfloat16
F32 = jnp.float32
VMEM = pl.BlockSpec(memory_space=pltpu.VMEM)
SMEM = pl.BlockSpec(memory_space=pltpu.SMEM)
ANY = pl.BlockSpec(memory_space=pl.ANY)
SMALL = pltpu.CompilerParams(vmem_limit_bytes=4 << 20)


def struct(shape, dtype=BF):
    return jax.ShapeDtypeStruct(shape, dtype)


def dot(a, b, ca, cb):
    return lax.dot_general(a, b, (((ca,), (cb,)), ((), ())), preferred_element_type=F32)


def core_of_chip():
    return lax.rem(lax.axis_index("tensor"), 2)


def probs_of(query, key):
    scores = dot(query, key, 1, 1) * SCALE
    rows = lax.broadcasted_iota(jnp.int32, scores.shape, 0)
    cols = lax.broadcasted_iota(jnp.int32, scores.shape, 1)
    scores = jnp.where(rows >= cols, scores, -jnp.inf)
    top = jnp.max(scores, axis=1, keepdims=True)
    weights = jnp.exp(scores - top)
    return weights / jnp.sum(weights, axis=1, keepdims=True)


def forward_kernel(qkv_hbm, weight_hbm, own_hbm, theirs_hbm, qkv, weight, context, own, theirs, sems):
    half, width = theirs.shape
    depth = weight.shape[0] // 2
    load_qkv = pltpu.make_async_copy(qkv_hbm.at[0], qkv, sems.at[0])
    loads = [
        pltpu.make_async_copy(weight_hbm.at[0, part], weight.at[part], sems.at[1 + k])
        for k, part in enumerate((slice(0, depth), slice(depth, 2 * depth)))
    ]
    load_qkv.start()
    for load in loads:
        load.start()
    load_qkv.wait()
    for h in range(qkv.shape[2] // HD):
        c = slice(h * HD, (h + 1) * HD)
        probs = probs_of(qkv[0, :, c], qkv[1, :, c]).astype(BF)
        context[:, c] = dot(probs, qkv[2, :, c], 1, 0).astype(BF)
    core = core_of_chip()
    first = pl.multiple_of((1 - core) * half, half)
    second = pl.multiple_of(core * half, half)
    both = jnp.concatenate([context[pl.ds(first, half), :], context[pl.ds(second, half), :]], axis=0)
    for load in loads:
        load.wait()
    stores = []
    for n, c in enumerate((slice(0, width // 2), slice(width // 2, width))):
        product = dot(both, weight[:, c], 1, 0)
        theirs[:, c] = product[:half].astype(BF)
        own[:, c] = product[half:]
        for k, (near, far) in enumerate(((theirs, theirs_hbm), (own, own_hbm))):
            stores.append(pltpu.make_async_copy(near.at[:, c], far.at[:, c], sems.at[3 + 2 * n + k]))
            stores[-1].start()
    for store in stores:
        store.wait()


def aside_kernel(
    slots, stash, qkv, residual, grad_hbm, weight_hbm, pair, rows, grad_context, grad, weight, sems
):
    sections = lax.axis_size("pipe")
    partner = lax.rem(lax.axis_index("pipe") + sections // 2, sections)
    share = rows.shape[0]
    half = residual.shape[1] // 2
    first = core_of_chip() * half + lax.div(lax.axis_index("tensor"), 2) * share
    first = pl.multiple_of(first, share)
    copies = (
        pltpu.make_async_copy(grad_hbm.at[0], grad, sems.at[0]),
        pltpu.make_async_copy(weight_hbm.at[0], weight, sems.at[1]),
        pltpu.make_async_copy(stash.at[0, slots[partner]], pair.at[0], sems.at[2]),
        pltpu.make_async_copy(qkv.at[0], pair.at[1], sems.at[3]),
        pltpu.make_async_copy(residual.at[0, pl.ds(first, share)], rows, sems.at[4]),
    )
    for copy in copies:
        copy.start()
    for copy in copies:
        copy.wait()
    grad_context[...] = dot(grad[...], weight[...], 1, 1).astype(BF)


def place_kernel(other, block, *refs):
    out, sem = refs[-2:]
    half = block.shape[0]
    core = core_of_chip()
    first = pl.multiple_of((1 - core if other else core) * half, half)
    copy = pltpu.make_async_copy(block, out.at[0, pl.ds(first, half)], sem)
    copy.start()
    copy.wait()


def backward_kernel(pair, grad_context, grads, evicted):
    for h in range(grad_context.shape[1] // HD):
        c = slice(h * HD, (h + 1) * HD)
        query, key, value = pair[0, 0, :, c], pair[0, 1, :, c], pair[0, 2, :, c]
        grad = grad_context[:, c]
        probs = probs_of(query, key)
        grad_probs = dot(grad, value, 1, 1)
        delta = jnp.sum(probs * grad_probs, axis=1, keepdims=True)
        grad_scores = (probs * (grad_probs - delta)).astype(BF)
        grads[0, 0, :, c] = (dot(grad_scores, key, 1, 0) * SCALE).astype(BF)
        grads[0, 1, :, c] = (dot(grad_scores, query, 0, 0) * SCALE).astype(BF)
        grads[0, 2, :, c] = dot(probs.astype(BF), grad, 0, 0).astype(BF)
    evicted[0] = pair[1]


def shifted(block, axis, distance):
    count = lax.axis_size(axis)
    return lax.ppermute(block, axis, [((i - distance) % count, i) for i in range(count)])


def crossed(block):
    return lax.ppermute(block, "tensor", [(i, i ^ 1) for i in range(lax.axis_size("tensor"))])


def exchanged(blocks):
    members = lax.axis_size("tensor")
    groups = [list(range(core, members, 2)) for core in range(2)]
    return lax.all_to_all(blocks, "tensor", 0, 0, axis_index_groups=groups, tiled=True)


def step(residual, out_proj, attn_in, stash_slots, grad_in, stash_slot):
    sections, members = lax.axis_size("pipe"), lax.axis_size("tensor")
    rows, width = residual.shape[1:]
    chips, half, share = members // 2, rows // 2, rows // members
    own, theirs = pl.pallas_call(
        forward_kernel,
        out_shape=(struct((half, width), F32), struct((half, width))),
        in_specs=[ANY, ANY],
        out_specs=(ANY, ANY),
        scratch_shapes=[
            pltpu.VMEM(attn_in.shape[1:], BF),
            pltpu.VMEM(out_proj.shape[1:], BF),
            pltpu.VMEM((rows, out_proj.shape[1]), BF),
            pltpu.VMEM((half, width), F32),
            pltpu.VMEM((half, width), BF),
            pltpu.SemaphoreType.DMA((7,)),
        ],
        name="front",
    )(attn_in, out_proj)
    received = crossed(theirs)
    partial = (own + received.astype(F32)).astype(BF).reshape(chips, share, width)
    parts = exchanged(partial)
    pair, own_rows, grad_context = pl.pallas_call(
        aside_kernel,
        out_shape=(
            struct((2, *attn_in.shape[1:])),
            struct((share, width)),
            struct((rows, out_proj.shape[1])),
        ),
        in_specs=[SMEM, ANY, ANY, ANY, ANY, ANY],
        out_specs=(VMEM, VMEM, VMEM),
        scratch_shapes=[
            pltpu.VMEM(grad_in.shape[1:], BF),
            pltpu.VMEM(out_proj.shape[1:], BF),
            pltpu.SemaphoreType.DMA((5,)),
        ],
        name="aside",
    )(stash_slot, stash_slots, attn_in, residual, grad_in, out_proj)
    swapped = shifted(pair, "pipe", sections // 2)
    total = own_rows.astype(F32)
    for chip in range(chips):
        total = total + parts[chip].astype(F32)
    total = total.astype(BF)
    moved = shifted(total, "pipe", 1)
    copies = jnp.broadcast_to(moved[None], (chips, share, width))
    arrived = exchanged(copies).reshape(half, width)
    qkv_grad, evicted = pl.pallas_call(
        backward_kernel,
        out_shape=(struct(attn_in.shape), struct(attn_in.shape)),
        in_specs=[VMEM, VMEM],
        out_specs=(VMEM, VMEM),
        compiler_params=SMALL,
        name="back",
    )(swapped, grad_context)
    other = crossed(arrived)
    placed = pl.pallas_call(
        functools.partial(place_kernel, False),
        out_shape=struct(residual.shape),
        in_specs=[VMEM],
        out_specs=ANY,
        scratch_shapes=[pltpu.SemaphoreType.DMA],
        compiler_params=SMALL,
        name="place",
    )(arrived)
    fwd_out = pl.pallas_call(
        functools.partial(place_kernel, True),
        out_shape=struct(residual.shape),
        in_specs=[VMEM, ANY],
        out_specs=ANY,
        input_output_aliases={1: 0},
        scratch_shapes=[pltpu.SemaphoreType.DMA],
        compiler_params=SMALL,
        name="join",
    )(other, placed)
    return fwd_out, qkv_grad, evicted


def solution(mesh):
    in_specs = (
        P("pipe", None, None),
        P("pipe", "tensor", None),
        P("pipe", None, None, "tensor"),
        P("pipe", None, None, None, "tensor"),
        P("pipe", None, None),
        P(),
    )
    out_specs = (
        P("pipe", None, None),
        P("pipe", None, None, "tensor"),
        P("pipe", None, None, "tensor"),
    )
    return jax.shard_map(step, mesh=mesh, in_specs=in_specs, out_specs=out_specs, check_vma=False)
```

```python
import functools

import jax
import jax.numpy as jnp
from jax import lax
from jax.experimental import pallas as pl
from jax.experimental.pallas import tpu as pltpu
from jax.sharding import PartitionSpec as P


HD = 128
SCALE = HD ** (-0.5)
BF = jnp.bfloat16
F32 = jnp.float32
VMEM = pl.BlockSpec(memory_space=pltpu.VMEM)
SMEM = pl.BlockSpec(memory_space=pltpu.SMEM)
ANY = pl.BlockSpec(memory_space=pl.ANY)
HBM = pl.BlockSpec(memory_space=pltpu.HBM)
SMALL = pltpu.CompilerParams(vmem_limit_bytes=4 << 20)


def struct(shape, dtype=BF):
    return jax.ShapeDtypeStruct(shape, dtype)


def dot(a, b, ca, cb):
    return lax.dot_general(a, b, (((ca,), (cb,)), ((), ())), preferred_element_type=F32)


def core_of_chip():
    return lax.rem(lax.axis_index("tensor"), 2)


def probs_of(query, key):
    scores = dot(query, key, 1, 1) * SCALE
    rows = lax.broadcasted_iota(jnp.int32, scores.shape, 0)
    cols = lax.broadcasted_iota(jnp.int32, scores.shape, 1)
    scores = jnp.where(rows >= cols, scores, -jnp.inf)
    top = jnp.max(scores, axis=1, keepdims=True)
    weights = jnp.exp(scores - top)
    return weights / jnp.sum(weights, axis=1, keepdims=True)


def forward_kernel(qkv_hbm, weight_hbm, own, theirs_hbm, qkv, weight, context, theirs, sems):
    half, width = theirs.shape
    depth = weight.shape[0] // 2
    load_qkv = pltpu.make_async_copy(qkv_hbm.at[0], qkv, sems.at[0])
    loads = [
        pltpu.make_async_copy(weight_hbm.at[0, part], weight.at[part], sems.at[1 + k])
        for k, part in enumerate((slice(0, depth), slice(depth, 2 * depth)))
    ]
    load_qkv.start()
    for load in loads:
        load.start()
    load_qkv.wait()
    for h in range(qkv.shape[2] // HD):
        c = slice(h * HD, (h + 1) * HD)
        probs = probs_of(qkv[0, :, c], qkv[1, :, c]).astype(BF)
        context[:, c] = dot(probs, qkv[2, :, c], 1, 0).astype(BF)
    core = core_of_chip()
    first = pl.multiple_of((1 - core) * half, half)
    second = pl.multiple_of(core * half, half)
    both = jnp.concatenate([context[pl.ds(first, half), :], context[pl.ds(second, half), :]], axis=0)
    for load in loads:
        load.wait()
    stores = []
    for n, c in enumerate((slice(0, width // 2), slice(width // 2, width))):
        product = dot(both, weight[:, c], 1, 0)
        theirs[:, c] = product[:half].astype(BF)
        own[:, c] = product[half:]
        stores.append(pltpu.make_async_copy(theirs.at[:, c], theirs_hbm.at[:, c], sems.at[3 + n]))
        stores[-1].start()
    for store in stores:
        store.wait()


def pick_kernel(slots, stash, qkv, residual, pair, rows, sems):
    sections = lax.axis_size("pipe")
    partner = lax.rem(lax.axis_index("pipe") + sections // 2, sections)
    share = rows.shape[0]
    half = residual.shape[1] // 2
    first = core_of_chip() * half + lax.div(lax.axis_index("tensor"), 2) * share
    first = pl.multiple_of(first, share)
    copies = (
        pltpu.make_async_copy(stash.at[0, slots[partner]], pair.at[0], sems.at[0]),
        pltpu.make_async_copy(qkv.at[0], pair.at[1], sems.at[1]),
        pltpu.make_async_copy(residual.at[0, pl.ds(first, share)], rows, sems.at[2]),
    )
    for copy in copies:
        copy.start()
    for copy in copies:
        copy.wait()


def grad_kernel(grad_hbm, weight_hbm, out, grad, weight, sems):
    copies = (
        pltpu.make_async_copy(grad_hbm.at[0], grad, sems.at[0]),
        pltpu.make_async_copy(weight_hbm.at[0], weight, sems.at[1]),
    )
    for copy in copies:
        copy.start()
    for copy in copies:
        copy.wait()
    out[...] = dot(grad[...], weight[...], 1, 1).astype(BF)


def place_kernel(other, block, *refs):
    out, sem = refs[-2:]
    half = block.shape[0]
    core = core_of_chip()
    first = pl.multiple_of((1 - core if other else core) * half, half)
    copy = pltpu.make_async_copy(block, out.at[0, pl.ds(first, half)], sem)
    copy.start()
    copy.wait()


def backward_kernel(pair, grad_context, grads, evicted):
    for h in range(grad_context.shape[1] // HD):
        c = slice(h * HD, (h + 1) * HD)
        query, key, value = pair[0, 0, :, c], pair[0, 1, :, c], pair[0, 2, :, c]
        grad = grad_context[:, c]
        probs = probs_of(query, key)
        grad_probs = dot(grad, value, 1, 1)
        delta = jnp.sum(probs * grad_probs, axis=1, keepdims=True)
        grad_scores = (probs * (grad_probs - delta)).astype(BF)
        grads[0, 0, :, c] = (dot(grad_scores, key, 1, 0) * SCALE).astype(BF)
        grads[0, 1, :, c] = (dot(grad_scores, query, 0, 0) * SCALE).astype(BF)
        grads[0, 2, :, c] = dot(probs.astype(BF), grad, 0, 0).astype(BF)
    evicted[0] = pair[1]


def shifted(block, axis, distance):
    count = lax.axis_size(axis)
    return lax.ppermute(block, axis, [((i - distance) % count, i) for i in range(count)])


def crossed(block):
    return lax.ppermute(block, "tensor", [(i, i ^ 1) for i in range(lax.axis_size("tensor"))])


def exchanged(blocks):
    members = lax.axis_size("tensor")
    groups = [list(range(core, members, 2)) for core in range(2)]
    return lax.all_to_all(blocks, "tensor", 0, 0, axis_index_groups=groups, tiled=True)


def step(residual, out_proj, attn_in, stash_slots, grad_in, stash_slot):
    sections, members = lax.axis_size("pipe"), lax.axis_size("tensor")
    rows, width = residual.shape[1:]
    chips, half, share = members // 2, rows // 2, rows // members
    own, theirs = pl.pallas_call(
        forward_kernel,
        out_shape=(struct((half, width), F32), struct((half, width))),
        in_specs=[HBM, HBM],
        out_specs=(VMEM, HBM),
        scratch_shapes=[
            pltpu.VMEM(attn_in.shape[1:], BF),
            pltpu.VMEM(out_proj.shape[1:], BF),
            pltpu.VMEM((rows, out_proj.shape[1]), BF),
            pltpu.VMEM((half, width), BF),
            pltpu.SemaphoreType.DMA((5,)),
        ],
        compiler_params=pltpu.CompilerParams(vmem_limit_bytes=52 << 20),
        name="front",
    )(attn_in, out_proj)
    received = crossed(theirs)
    partial = (own + received.astype(F32)).astype(BF)
    partial = partial.reshape(chips, share, width)
    parts = exchanged(partial)
    pair, own_rows = pl.pallas_call(
        pick_kernel,
        out_shape=(struct((2, *attn_in.shape[1:])), struct((share, width))),
        in_specs=[SMEM, HBM, HBM, HBM],
        out_specs=(VMEM, VMEM),
        scratch_shapes=[pltpu.SemaphoreType.DMA((3,))],
        name="pick",
    )(stash_slot, stash_slots, attn_in, residual)
    swapped = shifted(pair, "pipe", sections // 2)
    grad_context = pl.pallas_call(
        grad_kernel,
        out_shape=struct((rows, out_proj.shape[1])),
        in_specs=[HBM, HBM],
        out_specs=VMEM,
        scratch_shapes=[
            pltpu.VMEM(grad_in.shape[1:], BF),
            pltpu.VMEM(out_proj.shape[1:], BF),
            pltpu.SemaphoreType.DMA((2,)),
        ],
        name="gctx",
    )(grad_in, out_proj)
    total = own_rows.astype(F32)
    for chip in range(chips):
        total = total + parts[chip].astype(F32)
    total = total.astype(BF)
    moved = shifted(total, "pipe", 1)
    copies = jnp.broadcast_to(moved[None], (chips, share, width))
    arrived = exchanged(copies).reshape(half, width)
    qkv_grad, evicted = pl.pallas_call(
        backward_kernel,
        out_shape=(struct(attn_in.shape), struct(attn_in.shape)),
        in_specs=[VMEM, VMEM],
        out_specs=(VMEM, VMEM),
        compiler_params=SMALL,
        name="back",
    )(swapped, grad_context)
    other = crossed(arrived)
    placed = pl.pallas_call(
        functools.partial(place_kernel, False),
        out_shape=struct(residual.shape),
        in_specs=[ANY],
        out_specs=HBM,
        scratch_shapes=[pltpu.SemaphoreType.DMA],
        compiler_params=SMALL,
        name="place",
    )(arrived)
    fwd_out = pl.pallas_call(
        functools.partial(place_kernel, True),
        out_shape=struct(residual.shape),
        in_specs=[ANY, HBM],
        out_specs=HBM,
        input_output_aliases={1: 0},
        scratch_shapes=[pltpu.SemaphoreType.DMA],
        compiler_params=SMALL,
        name="join",
    )(other, placed)
    return fwd_out, qkv_grad, evicted


def solution(mesh):
    in_specs = (
        P("pipe", None, None),
        P("pipe", "tensor", None),
        P("pipe", None, None, "tensor"),
        P("pipe", None, None, None, "tensor"),
        P("pipe", None, None),
        P(),
    )
    out_specs = (
        P("pipe", None, None),
        P("pipe", None, None, "tensor"),
        P("pipe", None, None, "tensor"),
    )
    return jax.shard_map(step, mesh=mesh, in_specs=in_specs, out_specs=out_specs, check_vma=False)
```

```python
import functools

import jax
import jax.numpy as jnp
from jax import lax
from jax.experimental import pallas as pl
from jax.experimental.pallas import tpu as pltpu
from jax.sharding import PartitionSpec as P


HD = 128
SCALE = HD ** (-0.5)
BF = jnp.bfloat16
F32 = jnp.float32
VMEM = pl.BlockSpec(memory_space=pltpu.VMEM)
SMEM = pl.BlockSpec(memory_space=pltpu.SMEM)
ANY = pl.BlockSpec(memory_space=pl.ANY)
HBM = pl.BlockSpec(memory_space=pltpu.HBM)
SMALL = pltpu.CompilerParams(vmem_limit_bytes=4 << 20)


def struct(shape, dtype=BF):
    return jax.ShapeDtypeStruct(shape, dtype)


def dot(a, b, ca, cb):
    return lax.dot_general(a, b, (((ca,), (cb,)), ((), ())), preferred_element_type=F32)


def core_of_chip():
    return lax.rem(lax.axis_index("tensor"), 2)


def probs_of(query, key):
    scores = dot(query, key, 1, 1) * SCALE
    rows = lax.broadcasted_iota(jnp.int32, scores.shape, 0)
    cols = lax.broadcasted_iota(jnp.int32, scores.shape, 1)
    scores = jnp.where(rows >= cols, scores, -jnp.inf)
    top = jnp.max(scores, axis=1, keepdims=True)
    weights = jnp.exp(scores - top)
    return weights / jnp.sum(weights, axis=1, keepdims=True)


def forward_kernel(qkv_hbm, weight_hbm, own, theirs_hbm, qkv, weight, context, theirs, sems):
    half, width = theirs.shape
    depth = weight.shape[0] // 2
    load_qkv = pltpu.make_async_copy(qkv_hbm.at[0], qkv, sems.at[0])
    loads = [
        pltpu.make_async_copy(weight_hbm.at[0, part], weight.at[part], sems.at[1 + k])
        for k, part in enumerate((slice(0, depth), slice(depth, 2 * depth)))
    ]
    load_qkv.start()
    for load in loads:
        load.start()
    load_qkv.wait()
    for h in range(qkv.shape[2] // HD):
        c = slice(h * HD, (h + 1) * HD)
        probs = probs_of(qkv[0, :, c], qkv[1, :, c]).astype(BF)
        context[:, c] = dot(probs, qkv[2, :, c], 1, 0).astype(BF)
    core = core_of_chip()
    first = pl.multiple_of((1 - core) * half, half)
    second = pl.multiple_of(core * half, half)
    both = jnp.concatenate([context[pl.ds(first, half), :], context[pl.ds(second, half), :]], axis=0)
    for load in loads:
        load.wait()
    stores = []
    for n, c in enumerate((slice(0, width // 2), slice(width // 2, width))):
        product = dot(both, weight[:, c], 1, 0)
        theirs[:, c] = product[:half].astype(BF)
        own[:, c] = product[half:]
        stores.append(pltpu.make_async_copy(theirs.at[:, c], theirs_hbm.at[:, c], sems.at[3 + n]))
        stores[-1].start()
    for store in stores:
        store.wait()


def pick_kernel(slots, stash, qkv, pair, sems):
    sections = lax.axis_size("pipe")
    partner = lax.rem(lax.axis_index("pipe") + sections // 2, sections)
    copies = (
        pltpu.make_async_copy(stash.at[0, slots[partner]], pair.at[0], sems.at[0]),
        pltpu.make_async_copy(qkv.at[0], pair.at[1], sems.at[1]),
    )
    for copy in copies:
        copy.start()
    for copy in copies:
        copy.wait()


def grad_kernel(grad_hbm, weight_hbm, out, grad, weight, sems):
    copies = (
        pltpu.make_async_copy(grad_hbm.at[0], grad, sems.at[0]),
        pltpu.make_async_copy(weight_hbm.at[0], weight, sems.at[1]),
    )
    for copy in copies:
        copy.start()
    for copy in copies:
        copy.wait()
    out[...] = dot(grad[...], weight[...], 1, 1).astype(BF)


def place_kernel(other, block, *refs):
    out, sems = refs[-2:]
    half = block.shape[0]
    core = core_of_chip()
    first = (1 - core if other else core) * half
    pieces = sems.shape[0]
    share = half // pieces
    copies = []
    for k in range(pieces):
        to = pl.ds(pl.multiple_of(first + k * share, share), share)
        copies.append(
            pltpu.make_async_copy(block.at[pl.ds(k * share, share)], out.at[0, to], sems.at[k])
        )
    for copy in copies:
        copy.start()
    for copy in copies:
        copy.wait()


def backward_kernel(pair, grad_context, grads, evicted):
    for h in range(grad_context.shape[1] // HD):
        c = slice(h * HD, (h + 1) * HD)
        query, key, value = pair[0, 0, :, c], pair[0, 1, :, c], pair[0, 2, :, c]
        grad = grad_context[:, c]
        probs = probs_of(query, key)
        grad_probs = dot(grad, value, 1, 1)
        delta = jnp.sum(probs * grad_probs, axis=1, keepdims=True)
        grad_scores = (probs * (grad_probs - delta)).astype(BF)
        grads[0, 0, :, c] = (dot(grad_scores, key, 1, 0) * SCALE).astype(BF)
        grads[0, 1, :, c] = (dot(grad_scores, query, 0, 0) * SCALE).astype(BF)
        grads[0, 2, :, c] = dot(probs.astype(BF), grad, 0, 0).astype(BF)
    evicted[0] = pair[1]


def shifted(block, axis, distance):
    count = lax.axis_size(axis)
    return lax.ppermute(block, axis, [((i - distance) % count, i) for i in range(count)])


def crossed(block):
    return lax.ppermute(block, "tensor", [(i, i ^ 1) for i in range(lax.axis_size("tensor"))])


def exchanged(blocks):
    members = lax.axis_size("tensor")
    groups = [list(range(core, members, 2)) for core in range(2)]
    return lax.all_to_all(blocks, "tensor", 0, 0, axis_index_groups=groups, tiled=True)


def step(residual, out_proj, attn_in, stash_slots, grad_in, stash_slot):
    sections, members = lax.axis_size("pipe"), lax.axis_size("tensor")
    rows, width = residual.shape[1:]
    chips, half, share = members // 2, rows // 2, rows // members
    own, theirs = pl.pallas_call(
        forward_kernel,
        out_shape=(struct((half, width), F32), struct((half, width))),
        in_specs=[HBM, HBM],
        out_specs=(VMEM, HBM),
        scratch_shapes=[
            pltpu.VMEM(attn_in.shape[1:], BF),
            pltpu.VMEM(out_proj.shape[1:], BF),
            pltpu.VMEM((rows, out_proj.shape[1]), BF),
            pltpu.VMEM((half, width), BF),
            pltpu.SemaphoreType.DMA((5,)),
        ],
        compiler_params=pltpu.CompilerParams(vmem_limit_bytes=52 << 20),
        name="front",
    )(attn_in, out_proj)
    received = crossed(theirs)
    partial = (own + received.astype(F32)).astype(BF)
    partial = partial.reshape(chips, share, width)
    parts = exchanged(partial)
    pair = pl.pallas_call(
        pick_kernel,
        out_shape=struct((2, *attn_in.shape[1:])),
        in_specs=[SMEM, HBM, HBM],
        out_specs=VMEM,
        scratch_shapes=[pltpu.SemaphoreType.DMA((2,))],
        name="pick",
    )(stash_slot, stash_slots, attn_in)
    first = core_of_chip() * half + lax.div(lax.axis_index("tensor"), 2) * share
    own_rows = lax.dynamic_slice_in_dim(residual[0], first, share, 0).astype(F32)
    own_rows = lax.optimization_barrier(own_rows)
    swapped = shifted(pair, "pipe", sections // 2)
    grad_context = pl.pallas_call(
        grad_kernel,
        out_shape=struct((rows, out_proj.shape[1])),
        in_specs=[HBM, HBM],
        out_specs=VMEM,
        scratch_shapes=[
            pltpu.VMEM(grad_in.shape[1:], BF),
            pltpu.VMEM(out_proj.shape[1:], BF),
            pltpu.SemaphoreType.DMA((2,)),
        ],
        compiler_params=pltpu.CompilerParams(vmem_limit_bytes=52 << 20),
        name="gctx",
    )(grad_in, out_proj)
    total = own_rows
    for chip in range(chips):
        total = total + parts[chip].astype(F32)
    total = total.astype(BF)
    moved = shifted(total, "pipe", 1)
    copies = jnp.broadcast_to(moved[None], (chips, share, width))
    arrived = exchanged(copies).reshape(half, width)
    qkv_grad, evicted = pl.pallas_call(
        backward_kernel,
        out_shape=(struct(attn_in.shape), struct(attn_in.shape)),
        in_specs=[VMEM, VMEM],
        out_specs=(VMEM, VMEM),
        compiler_params=SMALL,
        name="back",
    )(swapped, grad_context)
    other = crossed(arrived)
    placed = pl.pallas_call(
        functools.partial(place_kernel, False),
        out_shape=struct(residual.shape),
        in_specs=[ANY],
        out_specs=HBM,
        scratch_shapes=[pltpu.SemaphoreType.DMA((4,))],
        compiler_params=SMALL,
        name="place",
    )(arrived)
    fwd_out = pl.pallas_call(
        functools.partial(place_kernel, True),
        out_shape=struct(residual.shape),
        in_specs=[ANY, HBM],
        out_specs=HBM,
        input_output_aliases={1: 0},
        scratch_shapes=[pltpu.SemaphoreType.DMA((4,))],
        compiler_params=SMALL,
        name="join",
    )(other, placed)
    return fwd_out, qkv_grad, evicted


def solution(mesh):
    in_specs = (
        P("pipe", None, None),
        P("pipe", "tensor", None),
        P("pipe", None, None, "tensor"),
        P("pipe", None, None, None, "tensor"),
        P("pipe", None, None),
        P(),
    )
    out_specs = (
        P("pipe", None, None),
        P("pipe", None, None, "tensor"),
        P("pipe", None, None, "tensor"),
    )
    return jax.shard_map(step, mesh=mesh, in_specs=in_specs, out_specs=out_specs, check_vma=False)
```

```python
import functools

import jax
import jax.numpy as jnp
from jax import lax
from jax.experimental import pallas as pl
from jax.experimental.pallas import tpu as pltpu
from jax.sharding import PartitionSpec as P


HD = 128
SCALE = HD ** (-0.5)
BF = jnp.bfloat16
F32 = jnp.float32
VMEM = pl.BlockSpec(memory_space=pltpu.VMEM)
SMEM = pl.BlockSpec(memory_space=pltpu.SMEM)
ANY = pl.BlockSpec(memory_space=pl.ANY)
HBM = pl.BlockSpec(memory_space=pltpu.HBM)
SMALL = pltpu.CompilerParams(vmem_limit_bytes=4 << 20)


def struct(shape, dtype=BF):
    return jax.ShapeDtypeStruct(shape, dtype)


def dot(a, b, ca, cb):
    return lax.dot_general(a, b, (((ca,), (cb,)), ((), ())), preferred_element_type=F32)


def core_of_chip():
    return lax.rem(lax.axis_index("tensor"), 2)


def probs_of(query, key):
    scores = dot(query, key, 1, 1) * SCALE
    rows = lax.broadcasted_iota(jnp.int32, scores.shape, 0)
    cols = lax.broadcasted_iota(jnp.int32, scores.shape, 1)
    scores = jnp.where(rows >= cols, scores, -jnp.inf)
    top = jnp.max(scores, axis=1, keepdims=True)
    weights = jnp.exp(scores - top)
    return weights / jnp.sum(weights, axis=1, keepdims=True)


def forward_kernel(qkv_hbm, weight_hbm, own, theirs, qkv, weight, context, sems):
    half, width = theirs.shape
    depth = weight.shape[0] // 2
    load_qkv = pltpu.make_async_copy(qkv_hbm.at[0], qkv, sems.at[0])
    loads = [
        pltpu.make_async_copy(weight_hbm.at[0, part], weight.at[part], sems.at[1 + k])
        for k, part in enumerate((slice(0, depth), slice(depth, 2 * depth)))
    ]
    load_qkv.start()
    for load in loads:
        load.start()
    load_qkv.wait()
    for h in range(qkv.shape[2] // HD):
        c = slice(h * HD, (h + 1) * HD)
        probs = probs_of(qkv[0, :, c], qkv[1, :, c]).astype(BF)
        context[:, c] = dot(probs, qkv[2, :, c], 1, 0).astype(BF)
    core = core_of_chip()
    first = pl.multiple_of((1 - core) * half, half)
    second = pl.multiple_of(core * half, half)
    both = jnp.concatenate([context[pl.ds(first, half), :], context[pl.ds(second, half), :]], axis=0)
    for load in loads:
        load.wait()
    for c in (slice(0, width // 2), slice(width // 2, width)):
        product = dot(both, weight[:, c], 1, 0)
        theirs[:, c] = product[:half].astype(BF)
        own[:, c] = product[half:]


def pick_kernel(slots, stash, qkv, pair, sems):
    sections = lax.axis_size("pipe")
    partner = lax.rem(lax.axis_index("pipe") + sections // 2, sections)
    copies = (
        pltpu.make_async_copy(stash.at[0, slots[partner]], pair.at[0], sems.at[0]),
        pltpu.make_async_copy(qkv.at[0], pair.at[1], sems.at[1]),
    )
    for copy in copies:
        copy.start()
    for copy in copies:
        copy.wait()


def grad_kernel(grad_hbm, weight_hbm, out, grad, weight, sems):
    copies = (
        pltpu.make_async_copy(grad_hbm.at[0], grad, sems.at[0]),
        pltpu.make_async_copy(weight_hbm.at[0], weight, sems.at[1]),
    )
    for copy in copies:
        copy.start()
    for copy in copies:
        copy.wait()
    out[...] = dot(grad[...], weight[...], 1, 1).astype(BF)


def place_kernel(other, block, *refs):
    out, sems = refs[-2:]
    half = block.shape[0]
    core = core_of_chip()
    first = (1 - core if other else core) * half
    pieces = sems.shape[0]
    share = half // pieces
    copies = []
    for k in range(pieces):
        to = pl.ds(pl.multiple_of(first + k * share, share), share)
        copies.append(
            pltpu.make_async_copy(block.at[pl.ds(k * share, share)], out.at[0, to], sems.at[k])
        )
    for copy in copies:
        copy.start()
    for copy in copies:
        copy.wait()


def backward_kernel(pair, grad_context, grads, evicted):
    for h in range(grad_context.shape[1] // HD):
        c = slice(h * HD, (h + 1) * HD)
        query, key, value = pair[0, 0, :, c], pair[0, 1, :, c], pair[0, 2, :, c]
        grad = grad_context[:, c]
        probs = probs_of(query, key)
        grad_probs = dot(grad, value, 1, 1)
        delta = jnp.sum(probs * grad_probs, axis=1, keepdims=True)
        grad_scores = (probs * (grad_probs - delta)).astype(BF)
        grads[0, 0, :, c] = (dot(grad_scores, key, 1, 0) * SCALE).astype(BF)
        grads[0, 1, :, c] = (dot(grad_scores, query, 0, 0) * SCALE).astype(BF)
        grads[0, 2, :, c] = dot(probs.astype(BF), grad, 0, 0).astype(BF)
    evicted[0] = pair[1]


def shifted(block, axis, distance):
    count = lax.axis_size(axis)
    return lax.ppermute(block, axis, [((i - distance) % count, i) for i in range(count)])


def crossed(block):
    return lax.ppermute(block, "tensor", [(i, i ^ 1) for i in range(lax.axis_size("tensor"))])


def exchanged(blocks):
    members = lax.axis_size("tensor")
    groups = [list(range(core, members, 2)) for core in range(2)]
    return lax.all_to_all(blocks, "tensor", 0, 0, axis_index_groups=groups, tiled=True)


def step(residual, out_proj, attn_in, stash_slots, grad_in, stash_slot):
    sections, members = lax.axis_size("pipe"), lax.axis_size("tensor")
    rows, width = residual.shape[1:]
    chips, half, share = members // 2, rows // 2, rows // members
    own, theirs = pl.pallas_call(
        forward_kernel,
        out_shape=(pltpu.VMEM((half, width), F32), pltpu.VMEM((half, width), BF)),
        in_specs=[HBM, HBM],
        out_specs=(VMEM, VMEM),
        scratch_shapes=[
            pltpu.VMEM(attn_in.shape[1:], BF),
            pltpu.VMEM(out_proj.shape[1:], BF),
            pltpu.VMEM((rows, out_proj.shape[1]), BF),
            pltpu.SemaphoreType.DMA((3,)),
        ],
        compiler_params=pltpu.CompilerParams(vmem_limit_bytes=53 << 20),
        name="front",
    )(attn_in, out_proj)
    received = crossed(theirs)
    partial = (own + received.astype(F32)).astype(BF)
    partial = partial.reshape(chips, share, width)
    parts = exchanged(partial)
    pair = pl.pallas_call(
        pick_kernel,
        out_shape=pltpu.VMEM((2, *attn_in.shape[1:]), BF),
        in_specs=[SMEM, HBM, HBM],
        out_specs=VMEM,
        scratch_shapes=[pltpu.SemaphoreType.DMA((2,))],
        name="pick",
    )(stash_slot, stash_slots, attn_in)
    first = core_of_chip() * half + lax.div(lax.axis_index("tensor"), 2) * share
    own_rows = lax.dynamic_slice_in_dim(residual[0], first, share, 0).astype(F32)
    own_rows = lax.optimization_barrier(own_rows)
    swapped = shifted(pair, "pipe", sections // 2)
    grad_context = pl.pallas_call(
        grad_kernel,
        out_shape=struct((rows, out_proj.shape[1])),
        in_specs=[HBM, HBM],
        out_specs=VMEM,
        scratch_shapes=[
            pltpu.VMEM(grad_in.shape[1:], BF),
            pltpu.VMEM(out_proj.shape[1:], BF),
            pltpu.SemaphoreType.DMA((2,)),
        ],
        compiler_params=pltpu.CompilerParams(vmem_limit_bytes=52 << 20),
        name="gctx",
    )(grad_in, out_proj)
    total = own_rows
    for chip in range(chips):
        total = total + parts[chip].astype(F32)
    total = total.astype(BF)
    moved = shifted(total, "pipe", 1)
    copies = jnp.broadcast_to(moved[None], (chips, share, width))
    arrived = exchanged(copies).reshape(half, width)
    qkv_grad, evicted = pl.pallas_call(
        backward_kernel,
        out_shape=(struct(attn_in.shape), struct(attn_in.shape)),
        in_specs=[VMEM, VMEM],
        out_specs=(VMEM, VMEM),
        compiler_params=SMALL,
        name="back",
    )(swapped, grad_context)
    other = crossed(arrived)
    placed = pl.pallas_call(
        functools.partial(place_kernel, False),
        out_shape=struct(residual.shape),
        in_specs=[ANY],
        out_specs=HBM,
        scratch_shapes=[pltpu.SemaphoreType.DMA((4,))],
        compiler_params=SMALL,
        name="place",
    )(arrived)
    fwd_out = pl.pallas_call(
        functools.partial(place_kernel, True),
        out_shape=struct(residual.shape),
        in_specs=[ANY, HBM],
        out_specs=HBM,
        input_output_aliases={1: 0},
        scratch_shapes=[pltpu.SemaphoreType.DMA((4,))],
        compiler_params=SMALL,
        name="join",
    )(other, placed)
    return fwd_out, qkv_grad, evicted


def solution(mesh):
    in_specs = (
        P("pipe", None, None),
        P("pipe", "tensor", None),
        P("pipe", None, None, "tensor"),
        P("pipe", None, None, None, "tensor"),
        P("pipe", None, None),
        P(),
    )
    out_specs = (
        P("pipe", None, None),
        P("pipe", None, None, "tensor"),
        P("pipe", None, None, "tensor"),
    )
    return jax.shard_map(
        step, mesh=mesh, in_specs=in_specs, out_specs=out_specs, check_vma=False
    )
```
